32 devices in a mesh: groups: 2 (over x), lon: 16 (over z, y, core).
Axes of the slice: x: 2, y: 2, z: 4, core: 2. Of those that a mesh axis runs over, the one named last changes fastest.
Arguments:
- fields: bfloat16 [32, 32, 1500], P(('groups', 'lon')), parts along dimension 0, may hold values from -6 to 6
- level_ids: int32 [6], P('groups'), parts along dimension 0, may hold values from 0 to 2, each once
- embed_weight: bfloat16 [500, 512], replicated, may hold values from -0.25 to 0.25
- level_embed: bfloat16 [3, 512], replicated, may hold values from -6 to 6
- enc_gain: float32 [512], replicated, may hold values from 0.1 to 1.9
- latent_query: bfloat16 [2, 512], replicated, may hold values from -0.049804688 to 0.049804688
- kv_weight: bfloat16 [512, 1024], replicated, may hold values from -0.25 to 0.25
- pool_out: bfloat16 [512, 512], replicated, may hold values from -0.25 to 0.25
- attn_gain: float32 [512], replicated, may hold values from 0.1 to 1.9
- qkv_weight: bfloat16 [512, 1536], replicated, may hold values from -0.25 to 0.25
- attn_proj: bfloat16 [512, 512], replicated, may hold values from -0.25 to 0.25
- mlp_gain: float32 [512], replicated, may hold values from 0.1 to 1.9
- mlp_up: bfloat16 [512, 2048], replicated, may hold values from -0.25 to 0.25
- mlp_down: bfloat16 [2048, 512], replicated, may hold values from -0.125 to 0.125
- level_mix: float32 [3, 2], replicated, may hold values from 0.25 to 4
- dec_gain: float32 [512], replicated, may hold values from 0.1 to 1.9
- dec_weight: bfloat16 [512, 500], replicated, may hold values from -0.25 to 0.25
Outputs:
- forecast: bfloat16 [32, 32, 1500], P(('groups', 'lon')), parts along dimension 0
The draws below stay inside these ranges and needn't reach their ends.
There are 2 independent parts, one for each index of `groups`. The reference program is written for one: setup_inputs(seed, part) draws one part's arguments, and reference() takes and returns one part's arrays. A program takes and returns all parts, laid end to end along the dimension named above; an argument that names none is the same for every part. Nothing has to cross between parts.
Inputs may be any that keep to these rules, and one draw needn't show every extreme that they name: level_ids holds each of 0 to 2 once.
All inputs are finite; a program needn't handle non-finite values.
Results may differ from the reference program's by a relative error of at most 0.014.
Values may be sent and summed in bfloat16 or wider, within the bound.
A program may use at most 128 MiB of HBM per device.

```python
import math
import jax
import jax.numpy as jnp
from jax import lax

D = 512
HEADS = 8
MLP = 2048
PIN = 500
LEV = 3
LATL = 2
W_LAT = 4
W_LON = 8
STEPS = 2
LON_DEV = 8
ROW_PARTS = 4
LAT_P = 4
LON_P = 128
N_LON = 16


def draw_fields(key, part):
    row_count = LAT_P * ROW_PARTS
    col_count = LON_P // ROW_PARTS
    scale_key = jax.random.fold_in(key, 11)
    value_key = jax.random.fold_in(key, 23)
    log_scales = jax.random.uniform(scale_key, (row_count, col_count, LEV, 1), jnp.float32, -1.5, 1.5)
    scales = jnp.exp(log_scales)
    base = jax.random.normal(value_key, (row_count, col_count, LEV, PIN), jnp.float32)
    values = jnp.clip(scales * base, -6.0, 6.0)
    return values.reshape(row_count, col_count, LEV * PIN).astype(jnp.bfloat16)


def normal_values(key, extent, scale, limit, kind=jnp.bfloat16):
    return jnp.clip(scale * jax.random.normal(key, extent, jnp.float32), -limit, limit).astype(kind)


def setup_inputs(seed: int = 0, part: int = 0) -> dict:
    arg_keys = jax.random.split(jax.random.key(seed), 18)
    own_keys = jax.random.split(jax.random.fold_in(arg_keys[17], part), 18)
    return {
        "fields": draw_fields(jax.random.fold_in(jax.random.fold_in(arg_keys[17], part), 71), part),
        "level_ids": jax.random.permutation(own_keys[1], LEV).astype(jnp.int32),
        "embed_weight": normal_values(arg_keys[2], (PIN, D), PIN ** -0.5, 0.25),
        "level_embed": normal_values(arg_keys[3], (LEV, D), 1.0, 6.0),
        "enc_gain": jnp.clip(1.0 + 0.18 * jax.random.normal(arg_keys[4], (D,), jnp.float32), 0.1, 1.9),
        "latent_query": jnp.clip(jax.random.uniform(arg_keys[5], (LATL, D), jnp.float32, -0.049804688, 0.049804688), -0.049804688, 0.049804688).astype(jnp.bfloat16),
        "kv_weight": normal_values(arg_keys[6], (D, 2 * D), D ** -0.5, 0.25),
        "pool_out": normal_values(arg_keys[7], (D, D), D ** -0.5, 0.25),
        "attn_gain": jnp.clip(1.0 + 0.18 * jax.random.normal(arg_keys[8], (D,), jnp.float32), 0.1, 1.9),
        "qkv_weight": normal_values(arg_keys[9], (D, 3 * D), D ** -0.5, 0.25),
        "attn_proj": normal_values(arg_keys[10], (D, D), D ** -0.5, 0.25),
        "mlp_gain": jnp.clip(1.0 + 0.18 * jax.random.normal(arg_keys[11], (D,), jnp.float32), 0.1, 1.9),
        "mlp_up": normal_values(arg_keys[12], (D, MLP), D ** -0.5, 0.25),
        "mlp_down": normal_values(arg_keys[13], (MLP, D), MLP ** -0.5, 0.125),
        "level_mix": jnp.clip(jnp.exp(jax.random.uniform(arg_keys[14], (LEV, LATL), jnp.float32, math.log(0.25), math.log(4.0))), 0.25, 4.0),
        "dec_gain": jnp.clip(1.0 + 0.18 * jax.random.normal(arg_keys[15], (D,), jnp.float32), 0.1, 1.9),
        "dec_weight": normal_values(arg_keys[16], (D, PIN), D ** -0.5, 0.25),
    }


norm_eps = 1e-05
head_eps = 1e-06

def product(einsum_form, left_side, right_side):
    return jnp.einsum(einsum_form, left_side.astype(jnp.float32), right_side.astype(jnp.float32))

def layer_norm(values, scale_row):
    average = lax.optimization_barrier(jnp.mean(values, axis=-1, keepdims=True))
    centred = values - average
    spread = lax.optimization_barrier(jnp.mean(centred * centred, axis=-1, keepdims=True))
    return centred * lax.rsqrt(spread + norm_eps) * scale_row

def unit_heads(values):
    shaped = values.reshape(values.shape[:-1] + (HEADS, D // HEADS))
    mean_square = lax.optimization_barrier(jnp.mean(shaped * shaped, axis=-1, keepdims=True))
    return (shaped * lax.rsqrt(mean_square + head_eps)).reshape(values.shape)

def level_tables(level_ids, level_embed, level_mix):
    picker = (level_ids[:, None] == jnp.arange(LEV, dtype=jnp.int32)[None, :]).astype(jnp.float32)
    embeds = jnp.dot(picker, level_embed.astype(jnp.float32), precision=lax.Precision.HIGHEST)
    mixing = jnp.dot(picker, level_mix, precision=lax.Precision.HIGHEST)
    return (embeds, mixing)

def encode(flat_fields, embeds, queries, embed_weight, enc_gain, kv_weight, pool_out, latent_query):
    head_dim = D // HEADS
    patch_count = flat_fields.shape[0]
    patches = flat_fields.reshape(patch_count * LEV, PIN)
    tokens = jnp.dot(patches, embed_weight, preferred_element_type=jnp.float32).reshape(patch_count, LEV, D)
    tokens = layer_norm(tokens + embeds[None], enc_gain).astype(jnp.bfloat16)
    keyval = jnp.dot(tokens.reshape(patch_count * LEV, D), kv_weight, preferred_element_type=jnp.float32)
    key_heads = unit_heads(keyval[:, :D]).astype(jnp.bfloat16).reshape(patch_count, LEV, HEADS, head_dim)
    value_heads = keyval[:, D:].astype(jnp.bfloat16).reshape(patch_count, LEV, HEADS, head_dim)
    scores = product('jhc,rlhc->rjhl', queries.reshape(LATL, HEADS, head_dim), key_heads) * head_dim ** (-0.5)
    weights = jnp.exp(scores)
    weights = (weights / lax.optimization_barrier(jnp.sum(weights, axis=-1, keepdims=True))).astype(jnp.bfloat16)
    pooled = product('rjhl,rlhc->rjhc', weights, value_heads).astype(jnp.bfloat16).reshape(patch_count * LATL, D)
    latents = jnp.dot(pooled, pool_out, preferred_element_type=jnp.float32).reshape(patch_count, LATL, D)
    return (latents + latent_query.astype(jnp.float32)[None]).astype(jnp.bfloat16)

def increments(backbone_out, embeds, mixing, dec_gain, dec_weight):
    patch_count = backbone_out.shape[0]
    blended = mixing[None, :, 0, None] * backbone_out[:, None, 0, :].astype(jnp.float32)
    for latent_index in range(1, LATL):
        blended = blended + mixing[None, :, latent_index, None] * backbone_out[:, None, latent_index, :].astype(jnp.float32)
    blended = blended + embeds[None]
    normed = layer_norm(blended, dec_gain).astype(jnp.bfloat16)
    result = jnp.dot(normed.reshape(patch_count * LEV, D), dec_weight, preferred_element_type=jnp.float32)
    return result.astype(jnp.bfloat16).reshape(patch_count, LEV * PIN)

def window_block(shifted, attn_gain, qkv_weight, attn_proj):
    head_dim = D // HEADS
    lat_count, lon_count = (shifted.shape[0], shifted.shape[1])
    lat_win, lon_win = (lat_count // W_LAT, lon_count // W_LON)
    inside = W_LAT * W_LON * LATL
    flat_tokens = shifted.reshape(-1, D)
    normed = layer_norm(flat_tokens.astype(jnp.float32), attn_gain).astype(jnp.bfloat16)
    projected = jnp.dot(normed, qkv_weight, preferred_element_type=jnp.float32)
    query_heads = unit_heads(projected[:, :D]).astype(jnp.bfloat16)
    key_heads = unit_heads(projected[:, D:2 * D]).astype(jnp.bfloat16)
    value_heads = projected[:, 2 * D:].astype(jnp.bfloat16)

    def to_windows(head_data):
        shaped = head_data.reshape(lat_win, W_LAT, lon_win, W_LON, LATL, HEADS, head_dim)
        return shaped.transpose(0, 2, 5, 1, 3, 4, 6).reshape(lat_win, lon_win, HEADS, inside, head_dim)
    scores = product('abhqc,abhkc->abhqk', to_windows(query_heads), to_windows(key_heads)) * head_dim ** (-0.5)
    row_index = jnp.arange(lat_count, dtype=jnp.int32).reshape(lat_win, W_LAT)
    region = (row_index >= lat_count - W_LAT // 2).astype(jnp.int32)
    region_tok = jnp.broadcast_to(region[:, :, None, None], (lat_win, W_LAT, W_LON, LATL)).reshape(lat_win, inside)
    allowed = (region_tok[:, :, None] == region_tok[:, None, :]).astype(jnp.float32)
    weights = jnp.exp(scores) * allowed[:, None, None, :, :]
    weights = (weights / lax.optimization_barrier(jnp.sum(weights, axis=-1, keepdims=True))).astype(jnp.bfloat16)
    win_mix = product('abhqk,abhkc->abhqc', weights, to_windows(value_heads)).astype(jnp.bfloat16)
    win_mix = win_mix.reshape(lat_win, lon_win, HEADS, W_LAT, W_LON, LATL, head_dim)
    win_mix = win_mix.transpose(0, 3, 1, 4, 5, 2, 6).reshape(-1, D)
    attended = flat_tokens.astype(jnp.float32) + jnp.dot(win_mix, attn_proj, preferred_element_type=jnp.float32)
    return attended.astype(jnp.bfloat16).reshape(shifted.shape)

def mlp_block(restored, mlp_gain, mlp_up, mlp_down):
    flat_tokens = restored.reshape(-1, D)
    normed = layer_norm(flat_tokens.astype(jnp.float32), mlp_gain).astype(jnp.bfloat16)
    hidden = jax.nn.gelu(jnp.dot(normed, mlp_up, preferred_element_type=jnp.float32)).astype(jnp.bfloat16)
    result = flat_tokens.astype(jnp.float32) + jnp.dot(hidden, mlp_down, preferred_element_type=jnp.float32)
    return result.astype(jnp.bfloat16).reshape(restored.shape)

def unfold_grid(folded):
    piece_cols = LON_DEV // ROW_PARTS
    shaped = folded.reshape(ROW_PARTS, LAT_P, N_LON, piece_cols, folded.shape[-1])
    return shaped.transpose(1, 2, 0, 3, 4).reshape(LAT_P, LON_P, folded.shape[-1])

def fold_grid(grid):
    piece_cols = LON_DEV // ROW_PARTS
    shaped = grid.reshape(LAT_P, N_LON, ROW_PARTS, piece_cols, grid.shape[-1])
    return shaped.transpose(2, 0, 1, 3, 4).reshape(LAT_P * ROW_PARTS, LON_P // ROW_PARTS, grid.shape[-1])

def reference(fields, level_ids, embed_weight, level_embed, enc_gain, latent_query, kv_weight, pool_out, attn_gain, qkv_weight, attn_proj, mlp_gain, mlp_up, mlp_down, level_mix, dec_gain, dec_weight):
    embeds, mixing = level_tables(level_ids, level_embed, level_mix)
    queries = unit_heads(latent_query.astype(jnp.float32)).astype(jnp.bfloat16)

    def encode_row(lat_row):
        return encode(lat_row, embeds, queries, embed_weight, enc_gain, kv_weight, pool_out, latent_query)

    def column_step(column_block):
        attended = window_block(column_block, attn_gain, qkv_weight, attn_proj)
        return mlp_block(attended, mlp_gain, mlp_up, mlp_down)

    def decode_row(lat_row):
        return increments(lat_row, embeds, mixing, dec_gain, dec_weight)
    current = unfold_grid(fields)
    for turn_index in range(STEPS):
        latents = lax.map(encode_row, current)
        shifted = jnp.roll(latents, (-(W_LAT // 2), -(W_LON // 2)), axis=(0, 1))
        columns = shifted.reshape(LAT_P, LON_P // W_LON, W_LON, LATL, D).transpose(1, 0, 2, 3, 4)
        backbone_out = lax.map(column_step, columns).transpose(1, 0, 2, 3, 4).reshape(LAT_P, LON_P, LATL, D)
        backbone_out = jnp.roll(backbone_out, (W_LAT // 2, W_LON // 2), axis=(0, 1))
        added = lax.map(decode_row, backbone_out)
        current = (current.astype(jnp.float32) + added.astype(jnp.float32)).astype(jnp.bfloat16)
    return fold_grid(current)
```

```python
import functools

import jax
import jax.numpy as jnp
from jax import lax
from jax.experimental import pallas as pl
from jax.experimental.pallas import tpu as pltpu
from jax.sharding import PartitionSpec as P

D = 512
HEADS = 8
HEAD = D // HEADS
HALF = D // 2
PIN = 500
PAD = 512
LEV = 3
LATL = 2
W_LAT = 4
W_LON = 8
STEPS = 2
ROW_PARTS = 4
WIN = W_LAT * W_LON
MESH = pl.DeviceIdType.MESH
F32 = jnp.float32
BF16 = jnp.bfloat16

norm_eps = 1e-05
head_eps = 1e-06


def mm(left, right):
    return jnp.dot(left, right, preferred_element_type=F32)


def layer_norm(values, scale_row):
    centred = values - jnp.mean(values, axis=-1, keepdims=True)
    spread = jnp.mean(centred * centred, axis=-1, keepdims=True)
    return centred * lax.rsqrt(spread + norm_eps) * scale_row


def head_sums(values, block):
    values = values.astype(BF16)
    return jnp.concatenate([mm(values[:, :HALF], block), mm(values[:, HALF:], block)], axis=1)


def kernel(
    n,
    lat_count,
    piece_cols,
    ids_ref,
    mix_ref,
    fields_ref,
    embed_ref,
    query_ref,
    enc_gain_ref,
    attn_gain_ref,
    mlp_gain_ref,
    dec_gain_ref,
    w_embed_hbm,
    w_kv_hbm,
    w_pool_hbm,
    w_qkv_hbm,
    w_proj_hbm,
    w_up_hbm,
    w_down_hbm,
    w_dec_hbm,
    out_ref,
    w_embed,
    w_kv,
    w_pool,
    w_qkv,
    w_proj,
    w_up,
    w_down,
    w_dec,
    rows32,
    work,
    send,
    recv,
    send_back,
    recv_back,
    weight_sem,
    send_sem,
    recv_sem,
    send_back_sem,
    recv_back_sem,
):
    me = lax.axis_index("lon")
    unroll = n <= 16
    lag = (W_LON // 2) // piece_cols
    half_rows = W_LAT // 2
    slots_win = WIN // piece_cols
    wide = LEV * PIN

    barrier = pltpu.get_barrier_semaphore()

    def greet(step, _):
        pl.semaphore_signal(
            barrier, inc=1, device_id={"lon": lax.rem(me + step, n)}, device_id_type=MESH
        )
        return 0

    lax.fori_loop(1, n, greet, 0, unroll=unroll)

    weights = [
        pltpu.make_async_copy(src, dst, weight_sem.at[i])
        for i, (src, dst) in enumerate(
            [
                (w_embed_hbm, w_embed),
                (w_kv_hbm, w_kv),
                (w_pool_hbm, w_pool),
                (w_qkv_hbm, w_qkv),
                (w_proj_hbm, w_proj),
                (w_up_hbm, w_up),
                (w_down_hbm, w_down),
                (w_dec_hbm, w_dec),
            ]
        )
    ]
    for copy in weights:
        copy.start()

    rows32[:, :wide] = fields_ref[0].astype(F32)

    group = 8 // piece_cols

    def pack(i, _):
        rows = rows32[pl.ds(pl.multiple_of(i * 8, 8), 8), :wide]
        for k in range(group):
            send[i * group + k] = rows[k * piece_cols : (k + 1) * piece_cols].astype(BF16)
        return 0

    lax.fori_loop(0, n // group, pack, 0, unroll=unroll)

    def place(device):
        piece = device // lat_count
        row = lax.rem(device, lat_count)
        shifted_row = lax.rem(row - half_rows + lat_count, lat_count)
        slot = shifted_row * ROW_PARTS + piece
        carry = (piece - lag + ROW_PARTS) // ROW_PARTS - 1
        return slot, carry

    my_slot, my_carry = place(me)

    pl.semaphore_wait(barrier, n - 1)

    def outward(step):
        target = lax.rem(me + step, n)
        return pltpu.make_async_remote_copy(
            src_ref=send.at[lax.rem(target - my_carry + n, n)],
            dst_ref=recv.at[my_slot],
            send_sem=send_sem,
            recv_sem=recv_sem,
            device_id={"lon": target},
            device_id_type=MESH,
        )

    def start_outward(step, _):
        outward(step).start()
        return 0

    lax.fori_loop(1, n, start_outward, 0, unroll=unroll)
    recv[my_slot] = send[lax.rem(me - my_carry + n, n)]

    embeds, mixes = [], []
    for l in range(LEV):
        row = jnp.zeros((1, D), F32)
        for k in range(LEV):
            hit = (ids_ref[l] == k).astype(F32)
            row = row + hit * embed_ref[k : k + 1, :].astype(F32)
        embeds.append(row)
        weights_l = []
        for j in range(LATL):
            total = jnp.float32(0.0)
            for k in range(LEV):
                total = total + (ids_ref[l] == k).astype(F32) * mix_ref[k, j]
            weights_l.append(total)
        mixes.append(weights_l)
    block = (
        lax.broadcasted_iota(jnp.int32, (HALF, HALF), 0) // HEAD
        == lax.broadcasted_iota(jnp.int32, (HALF, HALF), 1) // HEAD
    ).astype(BF16)
    query = query_ref[...].astype(F32)
    query_square = jnp.concatenate([query * query, jnp.zeros((6, D), F32)], axis=0)
    q_scale = lax.rsqrt(head_sums(query_square, block)[:LATL] * (1.0 / HEAD) + head_eps)
    q_unit = (query * q_scale).astype(BF16).astype(F32) * (HEAD**-0.5)

    def all_of(buffer, sem):
        part = buffer.at[pl.ds(0, n - 1)]
        return pltpu.make_async_copy(part, part, sem)

    all_of(recv, recv_sem).wait()

    lane = lax.broadcasted_iota(jnp.int32, (WIN, LEV * PAD), 1)

    def window(w, first):
        for i in range(slots_win):
            work[i * piece_cols : (i + 1) * piece_cols, :wide] = recv[w * slots_win + i].astype(F32)
        if first:
            weights[0].wait()
        flat = work[...]
        levels = [flat[:, :PIN]]
        for l in range(1, LEV):
            moved = pltpu.roll(flat, (PAD - PIN) * l, axis=1)
            levels.append(moved[:, l * PAD : l * PAD + PIN])
        current = jnp.concatenate(levels, axis=0).astype(BF16)

        shape = (LATL * WIN, HALF)
        token = lax.rem(lax.broadcasted_iota(jnp.int32, shape, 0), WIN)
        other = lax.rem(lax.broadcasted_iota(jnp.int32, shape, 1), WIN)
        edge = lat_count - half_rows
        region = (w * W_LAT + token // W_LON >= edge).astype(jnp.int32)
        region_other = (w * W_LAT + other // W_LON >= edge).astype(jnp.int32)
        allowed = (region == region_other).astype(F32)

        for step in range(STEPS):
            head = first and step == 0
            tokens = mm(current, w_embed[...])
            tokens = jnp.concatenate(
                [tokens[l * WIN : (l + 1) * WIN] + embeds[l] for l in range(LEV)], axis=0
            )
            tokens = layer_norm(tokens, enc_gain_ref[...]).astype(BF16)
            if head:
                weights[1].wait()
            keyval = mm(tokens, w_kv[...])
            keys, vals = keyval[:, :D], keyval[:, D:]
            k_scale = lax.rsqrt(head_sums(keys * keys, block) * (1.0 / HEAD) + head_eps)
            k_unit = keys * k_scale
            pooled = []
            for j in range(LATL):
                e = jnp.exp(head_sums(k_unit * q_unit[j : j + 1], block))
                top, bottom = 0.0, 0.0
                for l in range(LEV):
                    part = e[l * WIN : (l + 1) * WIN]
                    top = top + part * vals[l * WIN : (l + 1) * WIN]
                    bottom = bottom + part
                pooled.append(top / bottom)
            pooled = jnp.concatenate(pooled, axis=0).astype(BF16)
            if head:
                weights[2].wait()
            latents = mm(pooled, w_pool[...])
            latents = jnp.concatenate(
                [latents[j * WIN : (j + 1) * WIN] + query[j : j + 1] for j in range(LATL)], axis=0
            )
            latents = latents.astype(BF16).astype(F32)

            normed = layer_norm(latents, attn_gain_ref[...]).astype(BF16)
            if head:
                weights[3].wait()
            projected = mm(normed, w_qkv[...])
            wq, wk = projected[:, :D], projected[:, D : 2 * D]
            wv = projected[:, 2 * D :].astype(BF16)
            wq = wq * lax.rsqrt(head_sums(wq * wq, block) * (1.0 / HEAD) + head_eps)
            wk = wk * lax.rsqrt(head_sums(wk * wk, block) * (1.0 / HEAD) + head_eps)
            wq = (wq * (HEAD**-0.5)).astype(BF16)
            wk = wk.astype(BF16)
            mixed = []
            for s in range(2):
                side = slice(s * HALF, (s + 1) * HALF)
                big_k = jnp.concatenate([wk[:, side]] * (HALF // HEAD), axis=0) * block
                big_v = jnp.concatenate([wv[:, side]] * (HALF // HEAD), axis=0) * block
                scores = lax.dot_general(
                    wq[:, side], big_k, (((1,), (1,)), ((), ())), preferred_element_type=F32
                )
                e = (jnp.exp(scores) * allowed).astype(BF16)
                mixed.append(mm(e, big_v) / mm(e, block))
            mixed = jnp.concatenate(mixed, axis=1).astype(BF16)
            if head:
                weights[4].wait()
            attended = (latents + mm(mixed, w_proj[...])).astype(BF16).astype(F32)

            normed = layer_norm(attended, mlp_gain_ref[...]).astype(BF16)
            if head:
                weights[5].wait()
            hidden = jax.nn.gelu(mm(normed, w_up[...])).astype(BF16)
            if head:
                weights[6].wait()
            backbone = (attended + mm(hidden, w_down[...])).astype(BF16).astype(F32)

            blended = jnp.concatenate(
                [
                    mixes[l][0] * backbone[:WIN] + mixes[l][1] * backbone[WIN:] + embeds[l]
                    for l in range(LEV)
                ],
                axis=0,
            )
            decoded = layer_norm(blended, dec_gain_ref[...]).astype(BF16)
            if head:
                weights[7].wait()
            added = mm(decoded, w_dec[...]).astype(BF16)
            current = (current.astype(F32) + added.astype(F32)).astype(BF16)

        final = current.astype(F32)
        for l in range(LEV):
            work[:, l * PAD : l * PAD + PIN] = final[l * WIN : (l + 1) * WIN]
        flat = work[...]
        merged = flat
        for l in range(1, LEV):
            moved = pltpu.roll(flat, LEV * PAD - (PAD - PIN) * l, axis=1)
            merged = jnp.where(lane >= l * PIN, moved, merged)
        work[...] = merged
        for i in range(slots_win):
            send_back[w * slots_win + i] = work[
                i * piece_cols : (i + 1) * piece_cols, :wide
            ].astype(BF16)

    window(0, True)
    windows = lat_count // W_LAT
    if windows > 1:

        def more(w, _):
            window(w, False)
            return 0

        lax.fori_loop(1, windows, more, 0)

    def start_back(step, _):
        target = lax.rem(me + step, n)
        slot, carry = place(target)
        pltpu.make_async_remote_copy(
            src_ref=send_back.at[slot],
            dst_ref=recv_back.at[lax.rem(me - carry + n, n)],
            send_sem=send_back_sem,
            recv_sem=recv_back_sem,
            device_id={"lon": target},
            device_id_type=MESH,
        ).start()
        return 0

    lax.fori_loop(1, n, start_back, 0, unroll=unroll)
    recv_back[lax.rem(me - my_carry + n, n)] = send_back[my_slot]
    all_of(send, send_sem).wait()
    all_of(recv_back, recv_back_sem).wait()

    def unpack(i, _):
        rows = [recv_back[i * group + k].astype(F32) for k in range(group)]
        rows32[pl.ds(pl.multiple_of(i * 8, 8), 8), :wide] = jnp.concatenate(rows, axis=0)
        return 0

    lax.fori_loop(0, n // group, unpack, 0, unroll=unroll)
    out_ref[0] = rows32[:, :wide].astype(BF16)
    all_of(send_back, send_back_sem).wait()


def shards(
    n,
    fields,
    level_ids,
    embed_weight,
    level_embed,
    enc_gain,
    latent_query,
    kv_weight,
    pool_out,
    attn_gain,
    qkv_weight,
    attn_proj,
    mlp_gain,
    mlp_up,
    mlp_down,
    level_mix,
    dec_gain,
    dec_weight,
):
    local_count = fields.shape[1]
    wide = fields.shape[2]
    piece_cols = local_count // n
    lat_count = n // ROW_PARTS
    smem = pl.BlockSpec(memory_space=pltpu.SMEM)
    vmem = pl.BlockSpec(memory_space=pltpu.VMEM)
    any_space = pl.BlockSpec(memory_space=pl.ANY)
    matrices = (
        embed_weight,
        kv_weight,
        pool_out,
        qkv_weight,
        attn_proj,
        mlp_up,
        mlp_down,
        dec_weight,
    )
    return pl.pallas_call(
        functools.partial(kernel, n, lat_count, piece_cols),
        name="forecast",
        out_shape=jax.ShapeDtypeStruct(fields.shape, BF16),
        in_specs=[smem] * 2 + [vmem] * 7 + [any_space] * len(matrices),
        out_specs=vmem,
        scratch_shapes=[pltpu.VMEM(m.shape, BF16) for m in matrices]
        + [
            pltpu.VMEM((local_count, LEV * PAD), F32),
            pltpu.VMEM((WIN, LEV * PAD), F32),
            pltpu.VMEM((n, piece_cols, wide), BF16),
            pltpu.VMEM((n, piece_cols, wide), BF16),
            pltpu.VMEM((n, piece_cols, wide), BF16),
            pltpu.VMEM((n, piece_cols, wide), BF16),
            pltpu.SemaphoreType.DMA((len(matrices),)),
            pltpu.SemaphoreType.DMA,
            pltpu.SemaphoreType.DMA,
            pltpu.SemaphoreType.DMA,
            pltpu.SemaphoreType.DMA,
        ],
        compiler_params=pltpu.CompilerParams(
            collective_id=0, has_side_effects=True, vmem_limit_bytes=48 * 1024 * 1024
        ),
    )(
        level_ids,
        level_mix,
        fields,
        level_embed,
        latent_query,
        enc_gain.reshape(1, D),
        attn_gain.reshape(1, D),
        mlp_gain.reshape(1, D),
        dec_gain.reshape(1, D),
        *matrices,
    )


def solution(mesh):
    rep = P()
    rows = P(("groups", "lon"), None, None)
    return jax.shard_map(
        functools.partial(shards, mesh.shape["lon"]),
        mesh=mesh,
        in_specs=(rows, P("groups")) + (rep,) * 15,
        out_specs=rows,
        check_vma=False,
    )
```

```python
import functools

import jax
import jax.numpy as jnp
from jax import lax
from jax.experimental import pallas as pl
from jax.experimental.pallas import tpu as pltpu
from jax.sharding import PartitionSpec as P

D = 512
HEADS = 8
HEAD = D // HEADS
HALF = D // 2
PIN = 500
PAD = 512
LEV = 3
LATL = 2
W_LAT = 4
W_LON = 8
STEPS = 2
ROW_PARTS = 4
WIN = W_LAT * W_LON
MESH = pl.DeviceIdType.MESH
F32 = jnp.float32
BF16 = jnp.bfloat16

OPERANDS = (pltpu.VMEM, pltpu.SMEM, pltpu.SMEM) + (pltpu.VMEM,) * 14

norm_eps = 1e-05
head_eps = 1e-06


def mm(left, right):
    return jnp.dot(left, right, preferred_element_type=F32)


def layer_norm(values, scale_row):
    centred = values - jnp.mean(values, axis=-1, keepdims=True)
    spread = jnp.mean(centred * centred, axis=-1, keepdims=True)
    return centred * lax.rsqrt(spread + norm_eps) * scale_row


def head_sums(values, block):
    values = values.astype(BF16)
    return jnp.concatenate([mm(values[:, :HALF], block), mm(values[:, HALF:], block)], axis=1)


def kernel(
    n,
    lat_count,
    piece_cols,
    *refs,
):
    count = len(OPERANDS)
    sources, out_ref, landed, scratch = (
        refs[:count],
        refs[count],
        refs[count + 1 : 2 * count + 1],
        refs[2 * count + 1 :],
    )
    fields_ref, ids_ref, mix_ref, embed_ref, query_ref = landed[:5]
    enc_gain_ref, attn_gain_ref, mlp_gain_ref, dec_gain_ref = landed[5:9]
    w_embed, w_kv, w_pool, w_qkv, w_proj, w_up, w_down, w_dec = landed[9:]
    rows32, work, send, recv, send_back, recv_back = scratch[:6]
    load_sem, send_sem, recv_sem, send_back_sem, recv_back_sem = scratch[6:]

    me = lax.axis_index("lon")
    unroll = n <= 16
    lag = (W_LON // 2) // piece_cols
    half_rows = W_LAT // 2
    slots_win = WIN // piece_cols
    wide = LEV * PIN

    loads = [
        pltpu.make_async_copy(src, dst, load_sem.at[i])
        for i, (src, dst) in enumerate(zip(sources, landed))
    ]
    for copy in loads:
        copy.start()
    weights = loads[9:]

    barrier = pltpu.get_barrier_semaphore()

    def greet(step, _):
        pl.semaphore_signal(
            barrier, inc=1, device_id={"lon": lax.rem(me + step, n)}, device_id_type=MESH
        )
        return 0

    lax.fori_loop(1, n, greet, 0, unroll=unroll)

    loads[0].wait()
    rows32[:, :wide] = fields_ref[0].astype(F32)

    group = 8 // piece_cols

    def pack(i, _):
        rows = rows32[pl.ds(pl.multiple_of(i * 8, 8), 8), :wide]
        for k in range(group):
            send[i * group + k] = rows[k * piece_cols : (k + 1) * piece_cols].astype(BF16)
        return 0

    lax.fori_loop(0, n // group, pack, 0, unroll=unroll)

    def place(device):
        piece = device // lat_count
        row = lax.rem(device, lat_count)
        shifted_row = lax.rem(row - half_rows + lat_count, lat_count)
        slot = shifted_row * ROW_PARTS + piece
        carry = (piece - lag + ROW_PARTS) // ROW_PARTS - 1
        return slot, carry

    my_slot, my_carry = place(me)

    pl.semaphore_wait(barrier, n - 1)

    def outward(step):
        target = lax.rem(me + step, n)
        return pltpu.make_async_remote_copy(
            src_ref=send.at[lax.rem(target - my_carry + n, n)],
            dst_ref=recv.at[my_slot],
            send_sem=send_sem,
            recv_sem=recv_sem,
            device_id={"lon": target},
            device_id_type=MESH,
        )

    def start_outward(step, _):
        outward(step).start()
        return 0

    lax.fori_loop(1, n, start_outward, 0, unroll=unroll)
    recv[my_slot] = send[lax.rem(me - my_carry + n, n)]

    for copy in loads[1:9]:
        copy.wait()
    embeds, mixes = [], []
    for l in range(LEV):
        row = jnp.zeros((1, D), F32)
        for k in range(LEV):
            hit = (ids_ref[l] == k).astype(F32)
            row = row + hit * embed_ref[k : k + 1, :].astype(F32)
        embeds.append(row)
        weights_l = []
        for j in range(LATL):
            total = jnp.float32(0.0)
            for k in range(LEV):
                total = total + (ids_ref[l] == k).astype(F32) * mix_ref[j, k]
            weights_l.append(total)
        mixes.append(weights_l)
    block = (
        lax.broadcasted_iota(jnp.int32, (HALF, HALF), 0) // HEAD
        == lax.broadcasted_iota(jnp.int32, (HALF, HALF), 1) // HEAD
    ).astype(BF16)
    query = query_ref[...].astype(F32)
    query_square = jnp.concatenate([query * query, jnp.zeros((6, D), F32)], axis=0)
    q_scale = lax.rsqrt(head_sums(query_square, block)[:LATL] * (1.0 / HEAD) + head_eps)
    q_unit = (query * q_scale).astype(BF16).astype(F32) * (HEAD**-0.5)

    def all_of(buffer, sem):
        part = buffer.at[pl.ds(0, n - 1)]
        return pltpu.make_async_copy(part, part, sem)

    all_of(recv, recv_sem).wait()

    lane = lax.broadcasted_iota(jnp.int32, (WIN, LEV * PAD), 1)

    def window(w, first):
        for i in range(slots_win):
            work[i * piece_cols : (i + 1) * piece_cols, :wide] = recv[w * slots_win + i].astype(F32)
        if first:
            weights[0].wait()
        flat = work[...]
        levels = [flat[:, :PIN]]
        for l in range(1, LEV):
            moved = pltpu.roll(flat, (PAD - PIN) * l, axis=1)
            levels.append(moved[:, l * PAD : l * PAD + PIN])
        current = jnp.concatenate(levels, axis=0).astype(BF16)

        shape = (LATL * WIN, HALF)
        token = lax.rem(lax.broadcasted_iota(jnp.int32, shape, 0), WIN)
        other = lax.rem(lax.broadcasted_iota(jnp.int32, shape, 1), WIN)
        edge = lat_count - half_rows
        region = (w * W_LAT + token // W_LON >= edge).astype(jnp.int32)
        region_other = (w * W_LAT + other // W_LON >= edge).astype(jnp.int32)
        allowed = (region == region_other).astype(F32)

        for step in range(STEPS):
            head = first and step == 0
            tokens = mm(current, w_embed[...])
            tokens = jnp.concatenate(
                [tokens[l * WIN : (l + 1) * WIN] + embeds[l] for l in range(LEV)], axis=0
            )
            tokens = layer_norm(tokens, enc_gain_ref[...]).astype(BF16)
            if head:
                weights[1].wait()
            keyval = mm(tokens, w_kv[...])
            keys, vals = keyval[:, :D], keyval[:, D:]
            k_scale = lax.rsqrt(head_sums(keys * keys, block) * (1.0 / HEAD) + head_eps)
            k_unit = keys * k_scale
            pooled = []
            for j in range(LATL):
                e = jnp.exp(head_sums(k_unit * q_unit[j : j + 1], block))
                top, bottom = 0.0, 0.0
                for l in range(LEV):
                    part = e[l * WIN : (l + 1) * WIN]
                    top = top + part * vals[l * WIN : (l + 1) * WIN]
                    bottom = bottom + part
                pooled.append(top / bottom)
            pooled = jnp.concatenate(pooled, axis=0).astype(BF16)
            if head:
                weights[2].wait()
            latents = mm(pooled, w_pool[...])
            latents = jnp.concatenate(
                [latents[j * WIN : (j + 1) * WIN] + query[j : j + 1] for j in range(LATL)], axis=0
            )
            latents = latents.astype(BF16).astype(F32)

            normed = layer_norm(latents, attn_gain_ref[...]).astype(BF16)
            if head:
                weights[3].wait()
            projected = mm(normed, w_qkv[...])
            wq, wk = projected[:, :D], projected[:, D : 2 * D]
            wv = projected[:, 2 * D :].astype(BF16)
            wq = wq * lax.rsqrt(head_sums(wq * wq, block) * (1.0 / HEAD) + head_eps)
            wk = wk * lax.rsqrt(head_sums(wk * wk, block) * (1.0 / HEAD) + head_eps)
            wq = (wq * (HEAD**-0.5)).astype(BF16)
            wk = wk.astype(BF16)
            mixed = []
            for s in range(2):
                side = slice(s * HALF, (s + 1) * HALF)
                big_k = jnp.concatenate([wk[:, side]] * (HALF // HEAD), axis=0) * block
                big_v = jnp.concatenate([wv[:, side]] * (HALF // HEAD), axis=0) * block
                scores = lax.dot_general(
                    wq[:, side], big_k, (((1,), (1,)), ((), ())), preferred_element_type=F32
                )
                e = (jnp.exp(scores) * allowed).astype(BF16)
                mixed.append(mm(e, big_v) / mm(e, block))
            mixed = jnp.concatenate(mixed, axis=1).astype(BF16)
            if head:
                weights[4].wait()
            attended = (latents + mm(mixed, w_proj[...])).astype(BF16).astype(F32)

            normed = layer_norm(attended, mlp_gain_ref[...]).astype(BF16)
            if head:
                weights[5].wait()
            hidden = jax.nn.gelu(mm(normed, w_up[...])).astype(BF16)
            if head:
                weights[6].wait()
            backbone = (attended + mm(hidden, w_down[...])).astype(BF16).astype(F32)

            blended = jnp.concatenate(
                [
                    mixes[l][0] * backbone[:WIN] + mixes[l][1] * backbone[WIN:] + embeds[l]
                    for l in range(LEV)
                ],
                axis=0,
            )
            decoded = layer_norm(blended, dec_gain_ref[...]).astype(BF16)
            if head:
                weights[7].wait()
            added = lax.dot_general(
                decoded, w_dec[...], (((1,), (1,)), ((), ())), preferred_element_type=F32
            ).astype(BF16)
            current = (current.astype(F32) + added.astype(F32)).astype(BF16)

        final = current.astype(F32)
        for l in range(LEV):
            work[:, l * PAD : l * PAD + PIN] = final[l * WIN : (l + 1) * WIN]
        flat = work[...]
        merged = flat
        for l in range(1, LEV):
            moved = pltpu.roll(flat, LEV * PAD - (PAD - PIN) * l, axis=1)
            merged = jnp.where(lane >= l * PIN, moved, merged)
        work[...] = merged
        for i in range(slots_win):
            send_back[w * slots_win + i] = work[
                i * piece_cols : (i + 1) * piece_cols, :wide
            ].astype(BF16)

    window(0, True)
    windows = lat_count // W_LAT
    if windows > 1:

        def more(w, _):
            window(w, False)
            return 0

        lax.fori_loop(1, windows, more, 0)

    def start_back(step, _):
        target = lax.rem(me + step, n)
        slot, carry = place(target)
        pltpu.make_async_remote_copy(
            src_ref=send_back.at[slot],
            dst_ref=recv_back.at[lax.rem(me - carry + n, n)],
            send_sem=send_back_sem,
            recv_sem=recv_back_sem,
            device_id={"lon": target},
            device_id_type=MESH,
        ).start()
        return 0

    lax.fori_loop(1, n, start_back, 0, unroll=unroll)
    recv_back[lax.rem(me - my_carry + n, n)] = send_back[my_slot]
    all_of(send, send_sem).wait()
    all_of(recv_back, recv_back_sem).wait()

    def unpack(i, _):
        rows = [recv_back[i * group + k].astype(F32) for k in range(group)]
        rows32[pl.ds(pl.multiple_of(i * 8, 8), 8), :wide] = jnp.concatenate(rows, axis=0)
        return 0

    lax.fori_loop(0, n // group, unpack, 0, unroll=unroll)
    out_ref[0] = rows32[:, :wide].astype(BF16)
    all_of(send_back, send_back_sem).wait()


def shards(
    n,
    fields,
    level_ids,
    embed_weight,
    level_embed,
    enc_gain,
    latent_query,
    kv_weight,
    pool_out,
    attn_gain,
    qkv_weight,
    attn_proj,
    mlp_gain,
    mlp_up,
    mlp_down,
    level_mix,
    dec_gain,
    dec_weight,
):
    local_count = fields.shape[1]
    wide = fields.shape[2]
    piece_cols = local_count // n
    lat_count = n // ROW_PARTS
    operands = (
        fields,
        level_ids,
        level_mix.T,
        level_embed,
        latent_query,
        enc_gain.reshape(1, D),
        attn_gain.reshape(1, D),
        mlp_gain.reshape(1, D),
        dec_gain.reshape(1, D),
        embed_weight,
        kv_weight,
        pool_out,
        qkv_weight,
        attn_proj,
        mlp_up,
        mlp_down,
        dec_weight.T,
    )
    operands = tuple(pltpu.with_memory_space_constraint(x, pltpu.HBM) for x in operands)
    return pl.pallas_call(
        functools.partial(kernel, n, lat_count, piece_cols),
        name="forecast",
        out_shape=jax.ShapeDtypeStruct(fields.shape, BF16),
        in_specs=[pl.BlockSpec(memory_space=pltpu.HBM)] * len(operands),
        out_specs=pl.BlockSpec(memory_space=pltpu.VMEM),
        scratch_shapes=[
            space(x.shape, x.dtype) for space, x in zip(OPERANDS, operands, strict=True)
        ]
        + [
            pltpu.VMEM((local_count, LEV * PAD), F32),
            pltpu.VMEM((WIN, LEV * PAD), F32),
            pltpu.VMEM((n, piece_cols, wide), BF16),
            pltpu.VMEM((n, piece_cols, wide), BF16),
            pltpu.VMEM((n, piece_cols, wide), BF16),
            pltpu.VMEM((n, piece_cols, wide), BF16),
            pltpu.SemaphoreType.DMA((len(operands),)),
            pltpu.SemaphoreType.DMA,
            pltpu.SemaphoreType.DMA,
            pltpu.SemaphoreType.DMA,
            pltpu.SemaphoreType.DMA,
        ],
        compiler_params=pltpu.CompilerParams(
            collective_id=0, has_side_effects=True, vmem_limit_bytes=48 * 1024 * 1024
        ),
    )(*operands)


def solution(mesh):
    rep = P()
    rows = P(("groups", "lon"), None, None)
    return jax.shard_map(
        functools.partial(shards, mesh.shape["lon"]),
        mesh=mesh,
        in_specs=(rows, P("groups")) + (rep,) * 15,
        out_specs=rows,
        check_vma=False,
    )
```

```python
import functools

import jax
import jax.numpy as jnp
from jax import lax
from jax.experimental import pallas as pl
from jax.experimental.pallas import tpu as pltpu
from jax.sharding import PartitionSpec as P

D = 512
HEADS = 8
HEAD = D // HEADS
HALF = D // 2
PIN = 500
PAD = 512
LEV = 3
LATL = 2
W_LAT = 4
W_LON = 8
STEPS = 2
ROW_PARTS = 4
WIN = W_LAT * W_LON
MESH = pl.DeviceIdType.MESH
F32 = jnp.float32
BF16 = jnp.bfloat16

OPERANDS = (pltpu.VMEM, pltpu.SMEM, pltpu.SMEM) + (pltpu.VMEM,) * 14

norm_eps = 1e-05
head_eps = 1e-06


def mm(left, right):
    return jnp.dot(left, right, preferred_element_type=F32)


def layer_norm(values, scale_row):
    centred = values - jnp.mean(values, axis=-1, keepdims=True)
    spread = jnp.mean(centred * centred, axis=-1, keepdims=True)
    return centred * lax.rsqrt(spread + norm_eps) * scale_row


def head_sums(values, block):
    values = values.astype(BF16)
    return jnp.concatenate([mm(values[:, :HALF], block), mm(values[:, HALF:], block)], axis=1)


def kernel(
    n,
    lat_count,
    piece_cols,
    *refs,
):
    count = len(OPERANDS)
    sources, out_ref, landed, scratch = (
        refs[:count],
        refs[count],
        refs[count + 1 : 2 * count + 1],
        refs[2 * count + 1 :],
    )
    fields_ref, ids_ref, mix_ref, embed_ref, query_ref = landed[:5]
    enc_gain_ref, attn_gain_ref, mlp_gain_ref, dec_gain_ref = landed[5:9]
    w_embed, w_kv, w_pool, w_qkv, w_proj, w_up, w_down, w_dec = landed[9:]
    rows32, work, send, recv, send_back, recv_back = scratch[:6]
    w_dec_t, send_lat, recv_lat, lat_send_sem, lat_recv_sem = scratch[6:11]
    load_sem, send_sem, recv_sem, send_back_sem, recv_back_sem = scratch[11:]

    me = lax.axis_index("lon")
    unroll = n <= 16
    lag = (W_LON // 2) // piece_cols
    half_rows = W_LAT // 2
    slots_win = WIN // piece_cols
    wide = LEV * PIN

    barrier = pltpu.get_barrier_semaphore()

    def greet(step, _):
        pl.semaphore_signal(
            barrier, inc=1, device_id={"lon": lax.rem(me + step, n)}, device_id_type=MESH
        )
        return 0

    lax.fori_loop(1, n, greet, 0, unroll=unroll)

    loads = [
        pltpu.make_async_copy(src, dst, load_sem.at[i])
        for i, (src, dst) in enumerate(zip(sources, landed))
    ]
    for copy in loads:
        copy.start()
    weights = loads[9:]

    loads[0].wait()
    rows32[:, wide:] = jnp.zeros_like(rows32[:, wide:])
    rows32[:, :wide] = fields_ref[0].astype(F32)

    group = 8 // piece_cols

    def pack(i, _):
        rows = rows32[pl.ds(pl.multiple_of(i * 8, 8), 8), :]
        for k in range(group):
            send[i * group + k] = rows[k * piece_cols : (k + 1) * piece_cols].astype(BF16)
        return 0

    lax.fori_loop(0, n // group, pack, 0, unroll=unroll)

    def place(device):
        piece = device // lat_count
        row = lax.rem(device, lat_count)
        shifted_row = lax.rem(row - half_rows + lat_count, lat_count)
        slot = shifted_row * ROW_PARTS + piece
        carry = (piece - lag + ROW_PARTS) // ROW_PARTS - 1
        return slot, carry

    my_slot, my_carry = place(me)

    for copy in loads[1:9]:
        copy.wait()
    embeds, mixes = [], []
    for l in range(LEV):
        row = jnp.zeros((1, D), F32)
        for k in range(LEV):
            hit = (ids_ref[l] == k).astype(F32)
            row = row + hit * embed_ref[k : k + 1, :].astype(F32)
        embeds.append(row)
        weights_l = []
        for j in range(LATL):
            total = jnp.float32(0.0)
            for k in range(LEV):
                total = total + (ids_ref[l] == k).astype(F32) * mix_ref[j, k]
            weights_l.append(total)
        mixes.append(weights_l)
    block = (
        lax.broadcasted_iota(jnp.int32, (HALF, HALF), 0) // HEAD
        == lax.broadcasted_iota(jnp.int32, (HALF, HALF), 1) // HEAD
    ).astype(BF16)
    query = query_ref[...].astype(F32)
    query_square = jnp.concatenate([query * query, jnp.zeros((6, D), F32)], axis=0)
    q_scale = lax.rsqrt(head_sums(query_square, block)[:LATL] * (1.0 / HEAD) + head_eps)
    q_unit = (query * q_scale).astype(BF16).astype(F32) * (HEAD**-0.5)

    def split_levels(flat):
        levels = [flat[:, :PIN]]
        for l in range(1, LEV):
            moved = pltpu.roll(flat, (PAD - PIN) * l, axis=1)
            levels.append(moved[:, l * PAD : l * PAD + PIN])
        return jnp.concatenate(levels, axis=0).astype(BF16)

    def encode(current, head):
        if head:
            weights[0].wait()
        tokens = mm(current, w_embed[...])
        tokens = jnp.concatenate(
            [tokens[l * WIN : (l + 1) * WIN] + embeds[l] for l in range(LEV)], axis=0
        )
        tokens = layer_norm(tokens, enc_gain_ref[...]).astype(BF16)
        if head:
            weights[1].wait()
        keyval = mm(tokens, w_kv[...])
        keys, vals = keyval[:, :D], keyval[:, D:]
        k_scale = lax.rsqrt(head_sums(keys * keys, block) * (1.0 / HEAD) + head_eps)
        k_unit = keys * k_scale
        pooled = []
        for j in range(LATL):
            e = jnp.exp(head_sums(k_unit * q_unit[j : j + 1], block))
            top, bottom = 0.0, 0.0
            for l in range(LEV):
                part = e[l * WIN : (l + 1) * WIN]
                top = top + part * vals[l * WIN : (l + 1) * WIN]
                bottom = bottom + part
            pooled.append(top / bottom)
        pooled = jnp.concatenate(pooled, axis=0).astype(BF16)
        if head:
            weights[2].wait()
        latents = mm(pooled, w_pool[...])
        latents = jnp.concatenate(
            [latents[j * WIN : (j + 1) * WIN] + query[j : j + 1] for j in range(LATL)], axis=0
        )
        return latents.astype(BF16).astype(F32)


    def encode_home(c, head):
        rows = rows32[pl.ds(pl.multiple_of(c * WIN, WIN), WIN), :]
        latents = encode(split_levels(rows), head)
        latents = jnp.concatenate([latents[:WIN], latents[WIN:]], axis=1)
        for i in range(slots_win):
            block_rows = latents[i * piece_cols : (i + 1) * piece_cols]
            send_lat[c * slots_win + i] = block_rows.astype(BF16)

    encode_home(0, True)
    chunks = (n * piece_cols) // WIN
    if chunks > 1:

        def more_home(c, _):
            encode_home(c, False)
            return 0

        lax.fori_loop(1, chunks, more_home, 0)

    pl.semaphore_wait(barrier, n - 1)

    def send_out(source, target_buffer, sent, received):
        def one(step, _):
            target = lax.rem(me + step, n)
            pltpu.make_async_remote_copy(
                src_ref=source.at[lax.rem(target - my_carry + n, n)],
                dst_ref=target_buffer.at[my_slot],
                send_sem=sent,
                recv_sem=received,
                device_id={"lon": target},
                device_id_type=MESH,
            ).start()
            return 0

        lax.fori_loop(1, n, one, 0, unroll=unroll)
        target_buffer[my_slot] = source[lax.rem(me - my_carry + n, n)]

    send_out(send_lat, recv_lat, lat_send_sem, lat_recv_sem)
    send_out(send, recv, send_sem, recv_sem)

    def all_of(buffer, sem):
        part = buffer.at[pl.ds(0, n - 1)]
        return pltpu.make_async_copy(part, part, sem)

    weights[7].wait()
    w_dec_t[:, :PIN] = w_dec[...].T

    all_of(recv_lat, lat_recv_sem).wait()

    lane = lax.broadcasted_iota(jnp.int32, (WIN, LEV * PAD), 1)

    def window(w, first):
        for i in range(slots_win):
            part = recv_lat[w * slots_win + i].astype(F32)
            work[i * piece_cols : (i + 1) * piece_cols, : LATL * D] = part
        arrived = work[:, : LATL * D]
        shape = (LATL * WIN, HALF)
        token = lax.rem(lax.broadcasted_iota(jnp.int32, shape, 0), WIN)
        other = lax.rem(lax.broadcasted_iota(jnp.int32, shape, 1), WIN)
        edge = lat_count - half_rows
        region = (w * W_LAT + token // W_LON >= edge).astype(jnp.int32)
        region_other = (w * W_LAT + other // W_LON >= edge).astype(jnp.int32)
        allowed = (region == region_other).astype(F32)

        for step in range(STEPS):
            head = first and step == 0
            if step == 0:
                latents = jnp.concatenate([arrived[:, :D], arrived[:, D:]], axis=0)
            else:
                latents = encode(current, False)
            normed = layer_norm(latents, attn_gain_ref[...]).astype(BF16)
            if head:
                weights[3].wait()
            projected = mm(normed, w_qkv[...])
            wq, wk = projected[:, :D], projected[:, D : 2 * D]
            wv = projected[:, 2 * D :].astype(BF16)
            wq = wq * lax.rsqrt(head_sums(wq * wq, block) * (1.0 / HEAD) + head_eps)
            wk = wk * lax.rsqrt(head_sums(wk * wk, block) * (1.0 / HEAD) + head_eps)
            wq = (wq * (HEAD**-0.5)).astype(BF16)
            wk = wk.astype(BF16)
            mixed = []
            for s in range(2):
                side = slice(s * HALF, (s + 1) * HALF)
                big_k = jnp.concatenate([wk[:, side]] * (HALF // HEAD), axis=0) * block
                big_v = jnp.concatenate([wv[:, side]] * (HALF // HEAD), axis=0) * block
                scores = lax.dot_general(
                    wq[:, side], big_k, (((1,), (1,)), ((), ())), preferred_element_type=F32
                )
                e = (jnp.exp(scores) * allowed).astype(BF16)
                mixed.append(mm(e, big_v) / mm(e, block))
            mixed = jnp.concatenate(mixed, axis=1).astype(BF16)
            if head:
                weights[4].wait()
            attended = (latents + mm(mixed, w_proj[...])).astype(BF16).astype(F32)

            normed = layer_norm(attended, mlp_gain_ref[...]).astype(BF16)
            if head:
                weights[5].wait()
            hidden = jax.nn.gelu(mm(normed, w_up[...])).astype(BF16)
            if head:
                weights[6].wait()
            backbone = (attended + mm(hidden, w_down[...])).astype(BF16).astype(F32)

            blended = jnp.concatenate(
                [
                    mixes[l][0] * backbone[:WIN] + mixes[l][1] * backbone[WIN:] + embeds[l]
                    for l in range(LEV)
                ],
                axis=0,
            )
            decoded = layer_norm(blended, dec_gain_ref[...]).astype(BF16)
            added = mm(decoded, w_dec_t[:, :PIN]).astype(BF16)
            if step == 0:
                if first:
                    all_of(recv, recv_sem).wait()
                for i in range(slots_win):
                    part = recv[w * slots_win + i].astype(F32)
                    work[i * piece_cols : (i + 1) * piece_cols, :] = part
                current = split_levels(work[...])
            current = (current.astype(F32) + added.astype(F32)).astype(BF16)

        final = current.astype(F32)
        for l in range(LEV):
            work[:, l * PAD : l * PAD + PIN] = final[l * WIN : (l + 1) * WIN]
        flat = work[...]
        merged = flat
        for l in range(1, LEV):
            moved = pltpu.roll(flat, LEV * PAD - (PAD - PIN) * l, axis=1)
            merged = jnp.where(lane >= l * PIN, moved, merged)
        work[...] = merged
        for i in range(slots_win):
            send_back[w * slots_win + i] = work[
                i * piece_cols : (i + 1) * piece_cols, :
            ].astype(BF16)

    window(0, True)
    windows = lat_count // W_LAT
    if windows > 1:

        def more(w, _):
            window(w, False)
            return 0

        lax.fori_loop(1, windows, more, 0)

    def start_back(step, _):
        target = lax.rem(me + step, n)
        slot, carry = place(target)
        pltpu.make_async_remote_copy(
            src_ref=send_back.at[slot],
            dst_ref=recv_back.at[lax.rem(me - carry + n, n)],
            send_sem=send_back_sem,
            recv_sem=recv_back_sem,
            device_id={"lon": target},
            device_id_type=MESH,
        ).start()
        return 0

    lax.fori_loop(1, n, start_back, 0, unroll=unroll)
    recv_back[lax.rem(me - my_carry + n, n)] = send_back[my_slot]
    all_of(send, send_sem).wait()
    all_of(send_lat, lat_send_sem).wait()
    all_of(recv_back, recv_back_sem).wait()

    def unpack(i, _):
        rows = [recv_back[i * group + k].astype(F32) for k in range(group)]
        rows32[pl.ds(pl.multiple_of(i * 8, 8), 8), :] = jnp.concatenate(rows, axis=0)
        return 0

    lax.fori_loop(0, n // group, unpack, 0, unroll=unroll)
    out_ref[0] = rows32[:, :wide].astype(BF16)
    all_of(send_back, send_back_sem).wait()


def shards(
    n,
    fields,
    level_ids,
    embed_weight,
    level_embed,
    enc_gain,
    latent_query,
    kv_weight,
    pool_out,
    attn_gain,
    qkv_weight,
    attn_proj,
    mlp_gain,
    mlp_up,
    mlp_down,
    level_mix,
    dec_gain,
    dec_weight,
):
    local_count = fields.shape[1]
    piece_cols = local_count // n
    lat_count = n // ROW_PARTS
    operands = (
        fields,
        level_ids,
        level_mix.T,
        level_embed,
        latent_query,
        enc_gain.reshape(1, D),
        attn_gain.reshape(1, D),
        mlp_gain.reshape(1, D),
        dec_gain.reshape(1, D),
        embed_weight,
        kv_weight,
        pool_out,
        qkv_weight,
        attn_proj,
        mlp_up,
        mlp_down,
        dec_weight.T,
    )
    operands = tuple(pltpu.with_memory_space_constraint(x, pltpu.HBM) for x in operands)
    return pl.pallas_call(
        functools.partial(kernel, n, lat_count, piece_cols),
        name="forecast",
        out_shape=jax.ShapeDtypeStruct(fields.shape, BF16),
        in_specs=[pl.BlockSpec(memory_space=pltpu.HBM)] * len(operands),
        out_specs=pl.BlockSpec(memory_space=pltpu.VMEM),
        scratch_shapes=[
            space(x.shape, x.dtype) for space, x in zip(OPERANDS, operands, strict=True)
        ]
        + [
            pltpu.VMEM((local_count, LEV * PAD), F32),
            pltpu.VMEM((WIN, LEV * PAD), F32),
            pltpu.VMEM((n, piece_cols, LEV * PAD), BF16),
            pltpu.VMEM((n, piece_cols, LEV * PAD), BF16),
            pltpu.VMEM((n, piece_cols, LEV * PAD), BF16),
            pltpu.VMEM((n, piece_cols, LEV * PAD), BF16),
            pltpu.VMEM((D, PAD), BF16),
            pltpu.VMEM((n, piece_cols, LATL * D), BF16),
            pltpu.VMEM((n, piece_cols, LATL * D), BF16),
            pltpu.SemaphoreType.DMA,
            pltpu.SemaphoreType.DMA,
            pltpu.SemaphoreType.DMA((len(operands),)),
            pltpu.SemaphoreType.DMA,
            pltpu.SemaphoreType.DMA,
            pltpu.SemaphoreType.DMA,
            pltpu.SemaphoreType.DMA,
        ],
        compiler_params=pltpu.CompilerParams(
            collective_id=0, has_side_effects=True, vmem_limit_bytes=48 * 1024 * 1024
        ),
    )(*operands)


def solution(mesh):
    rep = P()
    rows = P(("groups", "lon"), None, None)
    return jax.shard_map(
        functools.partial(shards, mesh.shape["lon"]),
        mesh=mesh,
        in_specs=(rows, P("groups")) + (rep,) * 15,
        out_specs=rows,
        check_vma=False,
    )
```
